1024 devices in a mesh: clip: 64 (over z, y_hi), seq: 16 (over y_lo, x, core).
Axes of the slice: x: 4, y: 4 (y_hi: 2, y_lo: 2; y = y_hi * 2 + y_lo), z: 32, core: 2. Of those that a mesh axis runs over, the one named last changes fastest.
Arguments:
- features: bfloat16 [3, 64, 2048, 3072], P(None, 'clip', 'seq'), may hold values from -60 to 60
- disc_query: bfloat16 [3, 24, 16, 128], replicated, may hold values from -4 to 4
- value_map: bfloat16 [3, 128, 128], replicated, may hold values from -0.5 to 0.5
- disc_out: bfloat16 [3, 24, 16, 128], replicated, may hold values from -0.5 to 0.5
- label: int32 [64], P('clip'), may hold values from 0 to 1
Outputs:
- logits: float32 [64], P('clip')
- grad_query: float32 [3, 24, 16, 128], P(None, None, 'seq')
- grad_out: float32 [3, 24, 16, 128], P(None, None, 'seq')
- grad_value: float32 [3, 128, 128], P(None, 'seq')
The draws below stay inside these ranges and needn't reach their ends.
All inputs are finite; a program needn't handle non-finite values.
Results may differ from the reference program's by a relative error of at most 0.0095.
Values sent between devices are 32-bit elements; how exact they have to be, the bound alone decides.
No kernel may reach another device: no remote copies, remote signals or barrier semaphores. Data moves between devices by JAX's collectives and lax.ppermute only.
A program may use at most 64 MiB of HBM per device.

```python
import math
import jax
import jax.numpy as jnp
from jax import lax

HEADS = 24
HD = 128
TAPS = 3
NQ = 16
TOK_DEV = 128
DT = 3072
SEQ_LEN = 2048
CLIPS = 64
N_SEQ = 16


def draw_disc_query(key, part):
    result = jnp.clip(jax.random.normal(jax.random.fold_in(key, 12), (TAPS, HEADS, NQ, HD), jnp.float32), -4.0, 4.0)
    return result.astype(jnp.bfloat16)


def draw_features(key, part):
    full_shape = (TAPS, CLIPS, SEQ_LEN, DT)
    position = jnp.arange(SEQ_LEN, dtype=jnp.float32).reshape(1, 1, SEQ_LEN, 1)
    rising = 0.5 + position / max(SEQ_LEN - 1, 1)
    token_scale = jnp.exp(jax.random.uniform(jax.random.fold_in(key, 21), (TAPS, CLIPS, SEQ_LEN, 1), jnp.float32, math.log(0.3), math.log(3.0)))
    normal_part = jnp.clip(jax.random.normal(jax.random.fold_in(key, 25), full_shape, jnp.float32), -6.0, 6.0)
    result = normal_part * token_scale * rising
    return result.astype(jnp.bfloat16)


def touch_ends(values, own_key, smallest, high):
    index_at = [jax.random.randint(jax.random.fold_in(own_key, axis), (), 0, length) for axis, length in enumerate(values.shape)]
    longest = values.shape.index(max(values.shape))
    neighbour = index_at[:longest] + [(index_at[longest] + 1) % values.shape[longest]] + index_at[longest + 1:]
    return values.at[tuple(index_at)].set(smallest).at[tuple(neighbour)].set(high)


def gaussian(key, extent, deviation, most, kind=jnp.bfloat16):
    array = deviation * jax.random.normal(key, extent, jnp.float32)
    return jnp.clip(array, min=-most, max=most).astype(kind)


def setup_inputs(seed: int = 0) -> dict:
    seeds = jax.random.split(jax.random.key(seed), 6)
    return {
        "features": draw_features(jax.random.fold_in(seeds[5], 71), 0),
        "disc_query": draw_disc_query(jax.random.fold_in(seeds[5], 71), 0),
        "value_map": gaussian(seeds[2], (TAPS, HD, HD), HD ** -0.5, 0.5),
        "disc_out": gaussian(seeds[3], (TAPS, HEADS, NQ, HD), HD ** -0.5, 0.5),
        "label": touch_ends(jax.random.randint(seeds[4], (CLIPS,), 0, 2), jax.random.fold_in(seeds[4], 1), 0, 1).astype(jnp.int32),
    }


def rounded(array_in):
    return lax.optimization_barrier(array_in.astype(jnp.bfloat16)).astype(jnp.float32)

def reference(features, disc_query, value_map, disc_out, label):
    highest = lax.Precision.HIGHEST
    scaling = 0.5 / math.sqrt(HD)
    queries = disc_query.astype(jnp.float32)
    maps_wide = value_map.astype(jnp.float32)
    head_weights = disc_out.astype(jnp.float32)
    label_signs = 2.0 * label.astype(jnp.float32) - 1.0

    def one_clip(running, clip_index):
        clip_feats = lax.dynamic_index_in_dim(features, clip_index, axis=1, keepdims=False)
        label_sign = lax.dynamic_index_in_dim(label_signs, clip_index, axis=0, keepdims=False)
        kept_taps = []
        logit_value = jnp.zeros((), jnp.float32)
        for tap_index in range(TAPS):
            tap_feats = clip_feats[tap_index].astype(jnp.float32).reshape(SEQ_LEN, HEADS, HD)
            values_tap = rounded(jnp.einsum('she,ef->shf', tap_feats, maps_wide[tap_index], precision=highest))
            scores = jnp.einsum('hje,she->hjs', queries[tap_index], tap_feats, precision=highest) * scaling
            blocked = scores.reshape(HEADS, NQ, N_SEQ, TOK_DEV)
            block_max = lax.optimization_barrier(jnp.max(blocked, axis=-1))
            weights = jnp.exp(blocked - block_max[..., None])
            block_total = lax.optimization_barrier(jnp.sum(weights, axis=-1))
            block_acc = jnp.einsum('hjbt,bthf->hjbf', rounded(weights), values_tap.reshape(N_SEQ, TOK_DEV, HEADS, HD), precision=highest)
            overall = lax.optimization_barrier(jnp.max(block_max, axis=-1))
            factor = jnp.exp(block_max - overall[..., None])
            softmax_total = lax.optimization_barrier(jnp.sum(block_total * factor, axis=-1))
            output = lax.optimization_barrier(jnp.sum(block_acc * factor[..., None], axis=2)) / softmax_total[..., None]
            logit_value = logit_value + jnp.sum(output * head_weights[tap_index])
            kept_taps.append((tap_feats, values_tap, scores, overall, softmax_total, output))
        gradient_scale = -label_sign * jax.nn.sigmoid(-label_sign * logit_value)
        out_terms = []
        query_terms = []
        map_terms = []
        for tap_index in range(TAPS):
            tap_feats, values_tap, scores, overall, softmax_total, output = kept_taps[tap_index]
            upstream = rounded(gradient_scale * head_weights[tap_index])
            soft_weights = jnp.exp(scores - overall[..., None]) / softmax_total[..., None]
            value_dots = jnp.einsum('hje,she->hjs', upstream, values_tap, precision=highest)
            centre = lax.optimization_barrier(jnp.sum(output * upstream, axis=-1))
            slopes = soft_weights * (value_dots - centre[..., None])
            query_terms.append(scaling * jnp.einsum('hjs,she->hje', rounded(slopes), tap_feats, precision=highest))
            value_grads = rounded(jnp.einsum('hjs,hje->she', rounded(soft_weights), upstream, precision=highest))
            map_terms.append(jnp.einsum('she,shf->ef', tap_feats, value_grads, precision=highest))
            out_terms.append(gradient_scale * output)
        running = (running[0] + jnp.stack(out_terms), running[1] + jnp.stack(query_terms), running[2] + jnp.stack(map_terms))
        return (running, logit_value)
    start = (jnp.zeros((TAPS, HEADS, NQ, HD), jnp.float32), jnp.zeros((TAPS, HEADS, NQ, HD), jnp.float32), jnp.zeros((TAPS, HD, HD), jnp.float32))
    final, logits = lax.scan(one_clip, start, jnp.arange(CLIPS, dtype=jnp.int32))
    return (logits, final[1], final[0], final[2])
```

```python
import functools
import math

import jax
import jax.numpy as jnp
from jax import lax
from jax.experimental import pallas as pl
from jax.experimental.pallas import tpu as pltpu
from jax.sharding import Mesh, PartitionSpec as P

LANES = 128
GROUP = 8
F32 = jnp.float32
BF16 = jnp.bfloat16
ROWS_BY_COLUMNS = (((1,), (1,)), ((), ()))
VMEM_LARGE = 16 * 2**20
VMEM_SMALL = 16 * 2**20
ROWS_TO_COLUMNS = (((0,), (1,)), ((), ()))
OVER_ROWS = (((0,), (0,)), ((), ()))


def fetched(feats_hbm, feats, sem, groups, tap, group):
    width = GROUP * LANES
    part = tap * groups + group
    return pltpu.make_async_copy(
        feats_hbm.at[tap, 0, :, pl.ds(group * width, width)], feats.at[part], sem.at[part]
    )


def weights_kernel(
    groups, scaling, core, feats_hbm, query_hbm, map_hbm, weight_hbm, weights, ordered, stats,
    kept, masks, block_diag, feats, query, value_map, out_weight, sem, side_sem,
):
    taps, _, queries, _ = query.shape
    count = taps * groups
    half = LANES // 2
    each = queries // 2
    sides = [
        [
            pltpu.make_async_copy(whole.at[tap], copied.at[tap], side_sem.at[place, tap])
            for place, (whole, copied) in enumerate(((query_hbm, query), (weight_hbm, out_weight), (map_hbm, value_map)))
        ]
        for tap in range(taps)
    ]
    for tap in range(taps):
        for side in sides[tap]:
            side.start()
        for group in range(groups):
            fetched(feats_hbm, feats, sem, groups, tap, group).start()
    kept[...] = jnp.zeros_like(kept)
    mine = core[0]
    row = lax.broadcasted_iota(jnp.int32, (LANES, LANES), 0)
    column = lax.broadcasted_iota(jnp.int32, (LANES, LANES), 1)
    row_head = (row % half) // each
    parity = jnp.where(row < half, mine, 1 - mine)
    order = (column == row_head * queries + 2 * (row % each) + parity).astype(F32).astype(BF16)
    for head in range(GROUP):
        masks[head] = ((column % half) // each == head).astype(F32).astype(BF16)
    for tap in range(taps):
        for side in sides[tap]:
            side.wait()
        for group in range(groups):
            part = tap * groups + group
            heads = pl.ds(group * GROUP, GROUP)
            asked = lax.dot_general(
                query[tap, heads].reshape(LANES, LANES), order, ROWS_TO_COLUMNS, preferred_element_type=F32
            ).astype(BF16)
            wanted = jnp.dot(
                order, out_weight[tap, heads].reshape(LANES, LANES), preferred_element_type=F32
            ).astype(BF16)
            ordered[part] = wanted
            weighed = lax.dot_general(value_map[tap], wanted, ROWS_BY_COLUMNS, preferred_element_type=F32).astype(BF16)
            spread = block_diag.at[part % 3]
            for head in range(GROUP):
                columns = slice(head * LANES, (head + 1) * LANES)
                spread[columns, :LANES] = asked * masks[head]
                spread[columns, LANES:] = weighed * masks[head]
            fetched(feats_hbm, feats, sem, groups, tap, group).wait()
            both = jnp.dot(feats[part], spread[...], preferred_element_type=F32)
            scores = both[:, :LANES] * scaling
            dots = both[:, LANES:]
            top = jnp.max(scores, axis=0, keepdims=True)
            expo = jnp.exp(scores - top)
            total = jnp.sum(expo, axis=0, keepdims=True)
            weighted = jnp.sum(expo * dots, axis=0, keepdims=True)
            tilt = expo * (dots - weighted / total)
            kept[part : part + 1, :] = top
            kept[count + part : count + part + 1, :] = total
            kept[2 * count + part : 2 * count + part + 1, :] = weighted
            weights[part, 0] = expo.T.astype(BF16)
            weights[part, 1] = tilt.T.astype(BF16)
    found = kept[...]
    found = jnp.where(mine == 0, found, pltpu.roll(found, half, 1))
    stats[...] = jnp.broadcast_to(found[None], stats.shape)


def token_weights(core, features, disc_query, value_map, disc_out, scaling, members):
    taps, heads, queries, head_size = disc_query.shape
    groups = heads // GROUP
    tokens = features.shape[2]
    vmem = pl.BlockSpec(memory_space=pltpu.VMEM)
    return pl.pallas_call(
        functools.partial(weights_kernel, groups, scaling),
        out_shape=(
            jax.ShapeDtypeStruct((taps * groups, 2, LANES, tokens), BF16),
            jax.ShapeDtypeStruct((taps * groups, LANES, head_size), BF16),
            jax.ShapeDtypeStruct((members, 32, LANES), F32),
        ),
        in_specs=[pl.BlockSpec(memory_space=pltpu.SMEM)] + [pl.BlockSpec(memory_space=pl.ANY)] * 4,
        out_specs=(vmem, vmem, vmem),
        scratch_shapes=[
            pltpu.VMEM((32, LANES), F32),
            pltpu.VMEM((GROUP, LANES, LANES), BF16),
            pltpu.VMEM((3, GROUP * LANES, 2 * LANES), BF16),
            pltpu.VMEM((taps * groups, tokens, GROUP * LANES), BF16),
            pltpu.VMEM(disc_query.shape, BF16),
            pltpu.VMEM(value_map.shape, BF16),
            pltpu.VMEM(disc_out.shape, BF16),
            pltpu.SemaphoreType.DMA((taps * groups,)),
            pltpu.SemaphoreType.DMA((3, taps)),
        ],
        compiler_params=pltpu.CompilerParams(vmem_limit_bytes=VMEM_LARGE),
        cost_estimate=pl.CostEstimate(flops=7 * 10**8, bytes_accessed=4 * 10**6, transcendentals=10**5),
        name="token_weights",
    )(core, features, disc_query, value_map, disc_out)


def pooled_kernel(groups, feats_hbm, weights, sent, stays, feats, sem):
    count = weights.shape[0]
    taps = count // groups
    half = LANES // 2
    each = half // GROUP
    for tap in range(taps):
        for group in range(groups):
            fetched(feats_hbm, feats, sem, groups, tap, group).start()
    for tap in range(taps):
        for group in range(groups):
            part = tap * groups + group
            fetched(feats_hbm, feats, sem, groups, tap, group).wait()
            for head in range(GROUP):
                first = slice(head * each, (head + 1) * each)
                second = slice(half + head * each, half + (head + 1) * each)
                found = jnp.dot(
                    jnp.concatenate(
                        [weights[part, 0, first], weights[part, 0, second], weights[part, 1, first], weights[part, 1, second]],
                        axis=0,
                    ),
                    feats[part, :, head * LANES : (head + 1) * LANES],
                    preferred_element_type=F32,
                )
                sent[part, 0, first] = found[:each]
                sent[part, 1, first] = found[each : 2 * each]
                stays[part, first] = found[2 * each : 3 * each]
                sent[part, 2, first] = found[3 * each :]


def pooled_features(features, weights, groups):
    count, _, _, tokens = weights.shape
    vmem = pl.BlockSpec(memory_space=pltpu.VMEM)
    return pl.pallas_call(
        functools.partial(pooled_kernel, groups),
        out_shape=(
            jax.ShapeDtypeStruct((count, 3, LANES // 2, LANES), F32),
            jax.ShapeDtypeStruct((count, LANES // 2, LANES), F32),
        ),
        in_specs=[pl.BlockSpec(memory_space=pl.ANY), vmem],
        out_specs=(vmem, vmem),
        scratch_shapes=[
            pltpu.VMEM((count, tokens, GROUP * LANES), BF16),
            pltpu.SemaphoreType.DMA((count,)),
        ],
        compiler_params=pltpu.CompilerParams(vmem_limit_bytes=VMEM_LARGE),
        cost_estimate=pl.CostEstimate(flops=8 * 10**7, bytes_accessed=4 * 10**6, transcendentals=0),
        name="pooled_features",
    )(features, weights)


def joined_kernel(count, member_ref, core, label, every, logit_ref, coefficients):
    half = LANES // 2
    member, mine = member_ref[0], core[0]
    tops = every[:, 0:count]
    top = jnp.max(tops, axis=0)
    factors = jnp.exp(tops - top[None])
    total = jnp.sum(every[:, count : 2 * count] * factors, axis=0)
    centre = jnp.sum(every[:, 2 * count : 3 * count] * factors, axis=0) / total
    logit = jnp.sum(jnp.sum(centre, axis=1, keepdims=True), axis=0, keepdims=True)
    signs = jnp.full((1, 1), 2 * label[0] - 1, jnp.int32).astype(F32)
    slope = -signs * jax.nn.sigmoid(-signs * logit)
    logit_ref[...] = jnp.broadcast_to(logit, logit_ref.shape)
    padding = jnp.zeros((16 - count, LANES), F32)
    for place, of_member in enumerate((member, member + 1 - 2 * mine)):
        seen = every[of_member]
        share = slope * jnp.exp(seen[0:count] - top) / total
        moved = share * (centre - seen[2 * count : 3 * count] / seen[count : 2 * count])
        both = jnp.concatenate([share, padding, moved, padding], axis=0)
        coefficients[place] = jnp.where(mine == 0, both, pltpu.roll(both, half, 1)).T


def joined_stats(member, core, label, every, count):
    vmem = pl.BlockSpec(memory_space=pltpu.VMEM)
    smem = pl.BlockSpec(memory_space=pltpu.SMEM)
    return pl.pallas_call(
        functools.partial(joined_kernel, count),
        out_shape=(
            jax.ShapeDtypeStruct((8, LANES), F32),
            jax.ShapeDtypeStruct((2, LANES, 32), F32),
        ),
        in_specs=[smem, smem, smem, vmem],
        out_specs=(vmem, vmem),
        compiler_params=pltpu.CompilerParams(vmem_limit_bytes=VMEM_SMALL),
        cost_estimate=pl.CostEstimate(flops=10**10, bytes_accessed=10**8, transcendentals=10**5),
        name="joined_stats",
    )(member, core, label, every)


def scaled_kernel(groups, scaling, core, own, stays, other, coefficients, ordered, shares, whole):
    count = own.shape[0]
    taps = count // groups
    heads = groups * GROUP
    head_size = own.shape[3]
    half = LANES // 2
    each = half // GROUP
    mine = core[0]
    own_columns = coefficients[0]
    other_columns = coefficients[1]

    def spread(found, part, second):
        return jnp.broadcast_to(found[second * half : (second + 1) * half, part : part + 1], (half, LANES))

    for tap in range(taps):
        grad = jnp.zeros((head_size, head_size), F32)
        for group in range(groups):
            part = tap * groups + group
            first_pool = spread(own_columns, part, 0) * own[part, 0] + spread(other_columns, part, 0) * other[part, 1]
            second_pool = spread(own_columns, part, 1) * own[part, 1] + spread(other_columns, part, 1) * other[part, 0]
            tilt = scaling * (
                (spread(own_columns, part, 0) * stays[part] - spread(own_columns, 16 + part, 0) * own[part, 0])
                + (spread(other_columns, part, 0) * other[part, 2] - spread(other_columns, 16 + part, 0) * other[part, 1])
            )
            pool = jnp.concatenate([first_pool, second_pool], axis=0)
            high = pool.astype(BF16)
            low = (pool - high.astype(F32)).astype(BF16)
            grad = grad + lax.dot_general(high, ordered[part], OVER_ROWS, preferred_element_type=F32)
            grad = grad + lax.dot_general(low, ordered[part], OVER_ROWS, preferred_element_type=F32)
            row = tap * heads + group * GROUP
            for head in range(GROUP):
                rows = slice(head * each, (head + 1) * each)
                shares[0, :, row + head, :] = tilt[rows]
                shares[1, :, row + head, :] = first_pool[rows]
        pieces = shares.shape[1]
        kept = head_size // (2 * pieces)
        whole[tap] = grad.reshape(whole.shape[1:])
        place, second = divmod(tap, 2)
        row = taps * heads + second * kept
        shares[place, :, row : row + kept, :] = whole[tap, :, mine]
    row = taps * heads + kept
    shares[1, :, row:, :] = jnp.zeros((pieces, kept, head_size), F32)


def scaled_shares(core, own, stays, other, coefficients, ordered, taps, pieces, scaling):
    count, _, _, head_size = own.shape
    groups = count // taps
    kept = head_size // (2 * pieces)
    vmem = pl.BlockSpec(memory_space=pltpu.VMEM)
    smem = pl.BlockSpec(memory_space=pltpu.SMEM)
    rows = count * GROUP + 2 * kept
    return pl.pallas_call(
        functools.partial(scaled_kernel, groups, scaling),
        out_shape=jax.ShapeDtypeStruct((2, pieces, rows, head_size), F32),
        in_specs=[smem, vmem, vmem, vmem, vmem, vmem],
        out_specs=vmem,
        scratch_shapes=[pltpu.VMEM((taps, pieces, 2, kept, head_size), F32)],
        compiler_params=pltpu.CompilerParams(vmem_limit_bytes=VMEM_SMALL),
        cost_estimate=pl.CostEstimate(flops=10**8, bytes_accessed=3 * 10**6, transcendentals=10**5),
        name="scaled_shares",
    )(core, own, stays, other, coefficients, ordered)


def summed_kernel(terms, total):
    found = terms[0]
    for term in range(1, terms.shape[0]):
        found = found + terms[term]
    parts, rows, _ = total.shape
    if parts * rows > found.shape[0]:
        found = jnp.concatenate([found, jnp.zeros((parts * rows - found.shape[0], LANES), F32)], axis=0)
    total[...] = found.reshape(total.shape)


def summed_parts(terms, parts):
    rows = -(-terms.shape[1] // (8 * parts)) * 8
    vmem = pl.BlockSpec(memory_space=pltpu.VMEM)
    return pl.pallas_call(
        summed_kernel,
        out_shape=jax.ShapeDtypeStruct((parts, rows, LANES), F32),
        in_specs=[vmem],
        out_specs=vmem,
        compiler_params=pltpu.CompilerParams(vmem_limit_bytes=VMEM_SMALL),
        name="summed_parts",
    )(terms)


def repeated_kernel(terms, total):
    found = terms[0]
    for term in range(1, terms.shape[0]):
        found = found + terms[term]
    total[...] = jnp.broadcast_to(found[None], total.shape)


def repeated_sum(terms, copies):
    vmem = pl.BlockSpec(memory_space=pltpu.VMEM)
    return pl.pallas_call(
        repeated_kernel,
        out_shape=jax.ShapeDtypeStruct((copies, *terms.shape[1:]), F32),
        in_specs=[vmem],
        out_specs=vmem,
        compiler_params=pltpu.CompilerParams(vmem_limit_bytes=VMEM_SMALL),
        name="repeated_sum",
    )(terms)


def final_kernel(gathered, value_map, query_ref, out_ref, map_ref):
    taps, head_size, _ = value_map.shape
    each = query_ref.shape[0] // taps
    kept = map_ref.shape[1]
    parts = gathered.shape[0]
    first = jnp.concatenate([gathered[part, 0] for part in range(parts)], axis=0)
    second = jnp.concatenate([gathered[part, 1] for part in range(parts)], axis=0)
    query_ref[...] = first[: taps * each]
    for tap in range(taps):
        pool = second[tap * each : (tap + 1) * each]
        high = pool.astype(BF16)
        low = (pool - high.astype(F32)).astype(BF16)
        out_ref[tap * each : (tap + 1) * each, :] = jnp.dot(
            high, value_map[tap], preferred_element_type=F32
        ) + jnp.dot(low, value_map[tap], preferred_element_type=F32)
        row = taps * each + (tap % 2) * kept
        map_ref[tap] = (first, second)[tap // 2][row : row + kept]


def final_outputs(gathered, value_map, heads, kept):
    taps, head_size, _ = value_map.shape
    vmem = pl.BlockSpec(memory_space=pltpu.VMEM)
    each = jax.ShapeDtypeStruct((taps * heads, head_size), F32)
    return pl.pallas_call(
        final_kernel,
        out_shape=(each, each, jax.ShapeDtypeStruct((taps, kept, head_size), F32)),
        in_specs=[vmem, vmem],
        out_specs=(vmem, vmem, vmem),
        compiler_params=pltpu.CompilerParams(vmem_limit_bytes=VMEM_SMALL),
        name="final_outputs",
    )(gathered, value_map)


def exchanged(parts, axes):
    return lax.all_to_all(parts, axes, 0, 0)


SEQ = ("yl", "x", "core")
CLIP = ("zh", "zl", "yh")


def on_device(features, disc_query, value_map, disc_out, label):
    taps, heads, queries, head_size = disc_query.shape
    scaling = 0.5 / math.sqrt(head_size)
    members = lax.axis_size(SEQ)
    core = lax.axis_index("core").astype(jnp.int32).reshape(1)
    member = lax.axis_index(SEQ).astype(jnp.int32).reshape(1)
    features, disc_query, disc_out, map_there = (
        pltpu.with_memory_space_constraint(whole, pltpu.HBM) for whole in (features, disc_query, disc_out, value_map)
    )
    weights, ordered, stats = token_weights(core, features, disc_query, map_there, disc_out, scaling, members)
    every = exchanged(stats, SEQ)
    sent, stays = pooled_features(features, weights, heads // GROUP)
    other = lax.ppermute(sent, "core", [(0, 1), (1, 0)])
    logit, coefficients = joined_stats(member, core, label, every, ordered.shape[0])
    shares = scaled_shares(core, sent, stays, other, coefficients, ordered, taps, members // 2, scaling)
    terms = exchanged(shares.reshape(members, -1, head_size), ("yh", "yl", "x"))
    terms = exchanged(summed_parts(terms, lax.axis_size("zl")), ("zl",))
    terms = exchanged(repeated_sum(terms, lax.axis_size("zh")), ("zh",))
    terms = exchanged(repeated_sum(terms, 2 * lax.axis_size("zl")), ("zl", "yh"))
    gathered = terms.reshape(-1, 2, *terms.shape[1:])
    query_part, out_part, map_part = final_outputs(gathered, value_map, heads, head_size // members)
    return (
        logit[0, :1],
        query_part.reshape(taps, heads, 1, head_size),
        out_part.reshape(taps, heads, 1, head_size),
        map_part,
    )


def solution(mesh):
    clips, members = mesh.shape["clip"], mesh.shape["seq"]
    near = min(4, clips // 2)
    shape = (clips // (2 * near), near, 2, 2, members // 4, 2)
    inner = Mesh(mesh.devices.reshape(shape), (*CLIP, *SEQ))
    placed = (P(None, CLIP, SEQ, None), P(), P(), P(), P(CLIP))
    return jax.shard_map(
        on_device,
        mesh=inner,
        in_specs=placed,
        out_specs=(P(CLIP), P(None, None, SEQ, None), P(None, None, SEQ, None), P(None, SEQ, None)),
        check_vma=False,
    )
```

```python
import functools
import math

import jax
import jax.numpy as jnp
from jax import lax
from jax.experimental import pallas as pl
from jax.experimental.pallas import tpu as pltpu
from jax.sharding import Mesh, PartitionSpec as P

LANES = 128
GROUP = 8
F32 = jnp.float32
BF16 = jnp.bfloat16
ROWS_BY_COLUMNS = (((1,), (1,)), ((), ()))
AHEAD = 3
VMEM_LARGE = 16 * 2**20
VMEM_SMALL = 16 * 2**20
ROWS_TO_COLUMNS = (((0,), (1,)), ((), ()))
OVER_ROWS = (((0,), (0,)), ((), ()))


def fetched(feats_hbm, feats, sem, groups, tap, group):
    width = GROUP * LANES
    part = tap * groups + group
    return pltpu.make_async_copy(
        feats_hbm.at[tap, 0, :, pl.ds(group * width, width)], feats.at[part], sem.at[part]
    )


def weights_kernel(
    groups, scaling, core, feats_hbm, query_hbm, map_hbm, weight_hbm, weights, ordered, stats,
    kept, masks, block_diag, feats, query, value_map, out_weight, sem, side_sem,
):
    taps, _, queries, _ = query.shape
    count = taps * groups
    half = LANES // 2
    each = queries // 2
    sides = [
        [
            pltpu.make_async_copy(whole.at[tap], copied.at[tap], side_sem.at[place, tap])
            for place, (whole, copied) in enumerate(((query_hbm, query), (weight_hbm, out_weight), (map_hbm, value_map)))
        ]
        for tap in range(taps)
    ]
    for tap in range(taps):
        for side in sides[tap]:
            side.start()
    for tap in range(taps):
        for group in range(groups):
            fetched(feats_hbm, feats, sem, groups, tap, group).start()
    kept[...] = jnp.zeros_like(kept)
    mine = core[0]
    row = lax.broadcasted_iota(jnp.int32, (LANES, LANES), 0)
    column = lax.broadcasted_iota(jnp.int32, (LANES, LANES), 1)
    row_head = (row % half) // each
    parity = jnp.where(row < half, mine, 1 - mine)
    order = (column == row_head * queries + 2 * (row % each) + parity).astype(F32).astype(BF16)
    for head in range(GROUP):
        masks[head] = ((column % half) // each == head).astype(F32).astype(BF16)
    def prepare(part):
        tap, group = divmod(part, groups)
        heads = pl.ds(group * GROUP, GROUP)
        asked = lax.dot_general(
            query[tap, heads].reshape(LANES, LANES), order, ROWS_TO_COLUMNS, preferred_element_type=F32
        ).astype(BF16)
        wanted = jnp.dot(
            order, out_weight[tap, heads].reshape(LANES, LANES), preferred_element_type=F32
        ).astype(BF16)
        ordered[part] = wanted
        weighed = lax.dot_general(value_map[tap], wanted, ROWS_BY_COLUMNS, preferred_element_type=F32).astype(BF16)
        spread = block_diag.at[part % 3]
        for head in range(GROUP):
            rows = slice(head * LANES, (head + 1) * LANES)
            spread[rows, :LANES] = asked * masks[head]
            spread[rows, LANES:] = weighed * masks[head]

    for tap in range(taps):
        for side in sides[tap]:
            side.wait()
    for part in range(AHEAD):
        prepare(part)
    for part in range(count):
        fetched(feats_hbm, feats, sem, groups, *divmod(part, groups)).wait()
    for part in range(count):
        both = jnp.dot(feats[part], block_diag[part % 3], preferred_element_type=F32)
        if part + AHEAD < count:
            prepare(part + AHEAD)
        scores = both[:, :LANES] * scaling
        dots = both[:, LANES:]
        top = jnp.max(scores, axis=0, keepdims=True)
        expo = jnp.exp(scores - top)
        total = jnp.sum(expo, axis=0, keepdims=True)
        weighted = jnp.sum(expo * dots, axis=0, keepdims=True)
        tilt = expo * (dots - weighted / total)
        kept[part : part + 1, :] = top
        kept[count + part : count + part + 1, :] = total
        kept[2 * count + part : 2 * count + part + 1, :] = weighted
        weights[part, :, :LANES] = expo.astype(BF16)
        weights[part, :, LANES:] = tilt.astype(BF16)
    found = kept[...]
    found = jnp.where(mine == 0, found, pltpu.roll(found, half, 1))
    stats[...] = jnp.broadcast_to(found[None], stats.shape)


def token_weights(core, features, disc_query, value_map, disc_out, scaling, members):
    taps, heads, queries, head_size = disc_query.shape
    groups = heads // GROUP
    tokens = features.shape[2]
    vmem = pl.BlockSpec(memory_space=pltpu.VMEM)
    return pl.pallas_call(
        functools.partial(weights_kernel, groups, scaling),
        out_shape=(
            jax.ShapeDtypeStruct((taps * groups, tokens, 2 * LANES), BF16),
            jax.ShapeDtypeStruct((taps * groups, LANES, head_size), BF16),
            jax.ShapeDtypeStruct((members, 32, LANES), F32),
        ),
        in_specs=[pl.BlockSpec(memory_space=pltpu.SMEM)] + [pl.BlockSpec(memory_space=pl.ANY)] * 4,
        out_specs=(vmem, vmem, vmem),
        scratch_shapes=[
            pltpu.VMEM((32, LANES), F32),
            pltpu.VMEM((GROUP, LANES, LANES), BF16),
            pltpu.VMEM((3, GROUP * LANES, 2 * LANES), BF16),
            pltpu.VMEM((taps * groups, tokens, GROUP * LANES), BF16),
            pltpu.VMEM(disc_query.shape, BF16),
            pltpu.VMEM(value_map.shape, BF16),
            pltpu.VMEM(disc_out.shape, BF16),
            pltpu.SemaphoreType.DMA((taps * groups,)),
            pltpu.SemaphoreType.DMA((3, taps)),
        ],
        compiler_params=pltpu.CompilerParams(vmem_limit_bytes=VMEM_LARGE),
        cost_estimate=pl.CostEstimate(flops=7 * 10**8, bytes_accessed=4 * 10**6, transcendentals=10**5),
        name="token_weights",
    )(core, features, disc_query, value_map, disc_out)


def pooled_kernel(groups, feats_hbm, weights, sent, stays, feats, sem):
    count = weights.shape[0]
    taps = count // groups
    half = LANES // 2
    each = half // GROUP
    for tap in range(taps):
        for group in range(groups):
            fetched(feats_hbm, feats, sem, groups, tap, group).start()
    for tap in range(taps):
        for group in range(groups):
            fetched(feats_hbm, feats, sem, groups, tap, group).wait()
    for tap in range(taps):
        for group in range(groups):
            part = tap * groups + group
            rows = weights[part].T
            for head in range(GROUP):
                first = slice(head * each, (head + 1) * each)
                second = slice(half + head * each, half + (head + 1) * each)
                found = jnp.dot(
                    jnp.concatenate(
                        [rows[LANES * kind + half * place + head * each :][:each] for kind in range(2) for place in range(2)],
                        axis=0,
                    ),
                    feats[part, :, head * LANES : (head + 1) * LANES],
                    preferred_element_type=F32,
                )
                sent[part, 0, first] = found[:each]
                sent[part, 1, first] = found[each : 2 * each]
                stays[part, first] = found[2 * each : 3 * each]
                sent[part, 2, first] = found[3 * each :]


def pooled_features(features, weights, groups):
    count, tokens, _ = weights.shape
    vmem = pl.BlockSpec(memory_space=pltpu.VMEM)
    return pl.pallas_call(
        functools.partial(pooled_kernel, groups),
        out_shape=(
            jax.ShapeDtypeStruct((count, 3, LANES // 2, LANES), F32),
            jax.ShapeDtypeStruct((count, LANES // 2, LANES), F32),
        ),
        in_specs=[pl.BlockSpec(memory_space=pl.ANY), vmem],
        out_specs=(vmem, vmem),
        scratch_shapes=[
            pltpu.VMEM((count, tokens, GROUP * LANES), BF16),
            pltpu.SemaphoreType.DMA((count,)),
        ],
        compiler_params=pltpu.CompilerParams(vmem_limit_bytes=VMEM_LARGE),
        cost_estimate=pl.CostEstimate(flops=8 * 10**7, bytes_accessed=4 * 10**6, transcendentals=0),
        name="pooled_features",
    )(features, weights)


def joined_kernel(count, member_ref, core, label, every, logit_ref, coefficients):
    half = LANES // 2
    member, mine = member_ref[0], core[0]
    tops = every[:, 0:count]
    top = jnp.max(tops, axis=0)
    factors = jnp.exp(tops - top[None])
    total = jnp.sum(every[:, count : 2 * count] * factors, axis=0)
    centre = jnp.sum(every[:, 2 * count : 3 * count] * factors, axis=0) / total
    logit = jnp.sum(jnp.sum(centre, axis=1, keepdims=True), axis=0, keepdims=True)
    signs = jnp.full((1, 1), 2 * label[0] - 1, jnp.int32).astype(F32)
    slope = -signs * jax.nn.sigmoid(-signs * logit)
    logit_ref[...] = logit
    padding = jnp.zeros((16 - count, LANES), F32)
    for place, of_member in enumerate((member, member + 1 - 2 * mine)):
        seen = every[of_member]
        share = slope * jnp.exp(seen[0:count] - top) / total
        moved = share * (centre - seen[2 * count : 3 * count] / seen[count : 2 * count])
        both = jnp.concatenate([share, padding, moved, padding], axis=0)
        coefficients[place] = jnp.where(mine == 0, both, pltpu.roll(both, half, 1)).T


def joined_stats(member, core, label, every, count):
    vmem = pl.BlockSpec(memory_space=pltpu.VMEM)
    smem = pl.BlockSpec(memory_space=pltpu.SMEM)
    return pl.pallas_call(
        functools.partial(joined_kernel, count),
        out_shape=(
            jax.ShapeDtypeStruct((1, 1), F32),
            jax.ShapeDtypeStruct((2, LANES, 32), F32),
        ),
        in_specs=[smem, smem, smem, vmem],
        out_specs=(vmem, vmem),
        compiler_params=pltpu.CompilerParams(vmem_limit_bytes=VMEM_SMALL),
        cost_estimate=pl.CostEstimate(flops=10**10, bytes_accessed=10**8, transcendentals=10**5),
        name="joined_stats",
    )(member, core, label, every)


def scaled_kernel(groups, scaling, core, own, stays, other, coefficients, ordered, shares, whole):
    count = own.shape[0]
    taps = count // groups
    heads = groups * GROUP
    head_size = own.shape[3]
    half = LANES // 2
    each = half // GROUP
    mine = core[0]
    own_columns = coefficients[0]
    other_columns = coefficients[1]

    def spread(found, part, second):
        return jnp.broadcast_to(found[second * half : (second + 1) * half, part : part + 1], (half, LANES))

    for tap in range(taps):
        grad = jnp.zeros((head_size, head_size), F32)
        for group in range(groups):
            part = tap * groups + group
            first_pool = spread(own_columns, part, 0) * own[part, 0] + spread(other_columns, part, 0) * other[part, 1]
            second_pool = spread(own_columns, part, 1) * own[part, 1] + spread(other_columns, part, 1) * other[part, 0]
            tilt = scaling * (
                (spread(own_columns, part, 0) * stays[part] - spread(own_columns, 16 + part, 0) * own[part, 0])
                + (spread(other_columns, part, 0) * other[part, 2] - spread(other_columns, 16 + part, 0) * other[part, 1])
            )
            pool = jnp.concatenate([first_pool, second_pool], axis=0)
            high = pool.astype(BF16)
            low = (pool - high.astype(F32)).astype(BF16)
            grad = grad + lax.dot_general(high, ordered[part], OVER_ROWS, preferred_element_type=F32)
            grad = grad + lax.dot_general(low, ordered[part], OVER_ROWS, preferred_element_type=F32)
            row = tap * heads + group * GROUP
            for head in range(GROUP):
                rows = slice(head * each, (head + 1) * each)
                shares[0, :, row + head, :] = tilt[rows]
                shares[1, :, row + head, :] = first_pool[rows]
        pieces = shares.shape[1]
        kept = head_size // (2 * pieces)
        whole[tap] = grad.reshape(whole.shape[1:])
        place, second = divmod(tap, 2)
        row = taps * heads + second * kept
        shares[place, :, row : row + kept, :] = whole[tap, :, mine]
    row = taps * heads + kept
    shares[1, :, row:, :] = jnp.zeros((pieces, kept, head_size), F32)


def scaled_shares(core, own, stays, other, coefficients, ordered, taps, pieces, scaling):
    count, _, _, head_size = own.shape
    groups = count // taps
    kept = head_size // (2 * pieces)
    vmem = pl.BlockSpec(memory_space=pltpu.VMEM)
    smem = pl.BlockSpec(memory_space=pltpu.SMEM)
    rows = count * GROUP + 2 * kept
    return pl.pallas_call(
        functools.partial(scaled_kernel, groups, scaling),
        out_shape=jax.ShapeDtypeStruct((2, pieces, rows, head_size), F32),
        in_specs=[smem, vmem, vmem, vmem, vmem, vmem],
        out_specs=vmem,
        scratch_shapes=[pltpu.VMEM((taps, pieces, 2, kept, head_size), F32)],
        compiler_params=pltpu.CompilerParams(vmem_limit_bytes=VMEM_SMALL),
        cost_estimate=pl.CostEstimate(flops=10**8, bytes_accessed=3 * 10**6, transcendentals=10**5),
        name="scaled_shares",
    )(core, own, stays, other, coefficients, ordered)


def summed_kernel(terms, total):
    found = terms[0]
    for term in range(1, terms.shape[0]):
        found = found + terms[term]
    parts, rows, _ = total.shape
    if parts * rows > found.shape[0]:
        found = jnp.concatenate([found, jnp.zeros((parts * rows - found.shape[0], LANES), F32)], axis=0)
    total[...] = found.reshape(total.shape)


def summed_parts(terms, parts):
    rows = -(-terms.shape[1] // (8 * parts)) * 8
    vmem = pl.BlockSpec(memory_space=pltpu.VMEM)
    return pl.pallas_call(
        summed_kernel,
        out_shape=jax.ShapeDtypeStruct((parts, rows, LANES), F32),
        in_specs=[vmem],
        out_specs=vmem,
        compiler_params=pltpu.CompilerParams(vmem_limit_bytes=VMEM_SMALL),
        name="summed_parts",
    )(terms)


def repeated_kernel(terms, total):
    found = terms[0]
    for term in range(1, terms.shape[0]):
        found = found + terms[term]
    total[...] = jnp.broadcast_to(found[None], total.shape)


def repeated_sum(terms, copies):
    vmem = pl.BlockSpec(memory_space=pltpu.VMEM)
    return pl.pallas_call(
        repeated_kernel,
        out_shape=jax.ShapeDtypeStruct((copies, *terms.shape[1:]), F32),
        in_specs=[vmem],
        out_specs=vmem,
        compiler_params=pltpu.CompilerParams(vmem_limit_bytes=VMEM_SMALL),
        name="repeated_sum",
    )(terms)


def final_kernel(gathered, value_map, query_ref, out_ref, map_ref):
    taps, head_size, _ = value_map.shape
    each = query_ref.shape[0] // taps
    kept = map_ref.shape[1]
    parts = gathered.shape[0]
    first = jnp.concatenate([gathered[part, 0] for part in range(parts)], axis=0)
    second = jnp.concatenate([gathered[part, 1] for part in range(parts)], axis=0)
    query_ref[...] = first[: taps * each]
    for tap in range(taps):
        pool = second[tap * each : (tap + 1) * each]
        high = pool.astype(BF16)
        low = (pool - high.astype(F32)).astype(BF16)
        out_ref[tap * each : (tap + 1) * each, :] = jnp.dot(
            high, value_map[tap], preferred_element_type=F32
        ) + jnp.dot(low, value_map[tap], preferred_element_type=F32)
        row = taps * each + (tap % 2) * kept
        map_ref[tap] = (first, second)[tap // 2][row : row + kept]


def final_outputs(gathered, value_map, heads, kept):
    taps, head_size, _ = value_map.shape
    vmem = pl.BlockSpec(memory_space=pltpu.VMEM)
    each = jax.ShapeDtypeStruct((taps * heads, head_size), F32)
    return pl.pallas_call(
        final_kernel,
        out_shape=(each, each, jax.ShapeDtypeStruct((taps, kept, head_size), F32)),
        in_specs=[vmem, vmem],
        out_specs=(vmem, vmem, vmem),
        compiler_params=pltpu.CompilerParams(vmem_limit_bytes=VMEM_SMALL),
        name="final_outputs",
    )(gathered, value_map)


def exchanged(parts, axes):
    return lax.all_to_all(parts, axes, 0, 0)


SEQ = ("yl", "x", "core")
CLIP = ("zh", "zl", "yh")


def on_device(features, disc_query, value_map, disc_out, label):
    taps, heads, queries, head_size = disc_query.shape
    scaling = 0.5 / math.sqrt(head_size)
    members = lax.axis_size(SEQ)
    core = lax.axis_index("core").astype(jnp.int32).reshape(1)
    member = lax.axis_index(SEQ).astype(jnp.int32).reshape(1)
    features, disc_query, disc_out, map_there = (
        pltpu.with_memory_space_constraint(whole, pltpu.HBM) for whole in (features, disc_query, disc_out, value_map)
    )
    weights, ordered, stats = token_weights(core, features, disc_query, map_there, disc_out, scaling, members)
    every = exchanged(stats, SEQ)
    sent, stays = pooled_features(features, weights, heads // GROUP)
    other = lax.ppermute(sent, "core", [(0, 1), (1, 0)])
    logit, coefficients = joined_stats(member, core, label, every, ordered.shape[0])
    shares = scaled_shares(core, sent, stays, other, coefficients, ordered, taps, members // 2, scaling)
    terms = exchanged(shares.reshape(members, -1, head_size), ("yh", "yl", "x"))
    terms = exchanged(summed_parts(terms, lax.axis_size("zl")), ("zl",))
    terms = exchanged(repeated_sum(terms, lax.axis_size("zh")), ("zh",))
    terms = exchanged(repeated_sum(terms, 2 * lax.axis_size("zl")), ("zl", "yh"))
    gathered = terms.reshape(-1, 2, *terms.shape[1:])
    query_part, out_part, map_part = final_outputs(gathered, value_map, heads, head_size // members)
    return (
        logit.reshape(1),
        query_part.reshape(taps, heads, 1, head_size),
        out_part.reshape(taps, heads, 1, head_size),
        map_part,
    )


def solution(mesh):
    clips, members = mesh.shape["clip"], mesh.shape["seq"]
    near = min(4, clips // 2)
    shape = (clips // (2 * near), near, 2, 2, members // 4, 2)
    inner = Mesh(mesh.devices.reshape(shape), (*CLIP, *SEQ))
    placed = (P(None, CLIP, SEQ, None), P(), P(), P(), P(CLIP))
    return jax.shard_map(
        on_device,
        mesh=inner,
        in_specs=placed,
        out_specs=(P(CLIP), P(None, None, SEQ, None), P(None, None, SEQ, None), P(None, SEQ, None)),
        check_vma=False,
    )
```

```python
import functools
import math

import jax
import jax.numpy as jnp
from jax import lax
from jax.experimental import pallas as pl
from jax.experimental.pallas import tpu as pltpu
from jax.sharding import Mesh, PartitionSpec as P

LANES = 128
GROUP = 8
F32 = jnp.float32
BF16 = jnp.bfloat16
ROWS_BY_COLUMNS = (((1,), (1,)), ((), ()))
AHEAD = 3
VMEM_LARGE = 16 * 2**20
VMEM_SMALL = 16 * 2**20
ROWS_TO_COLUMNS = (((0,), (1,)), ((), ()))
OVER_ROWS = (((0,), (0,)), ((), ()))


def fetched(feats_hbm, feats, sem, groups, tap, group):
    width = GROUP * LANES
    part = tap * groups + group
    return pltpu.make_async_copy(
        feats_hbm.at[tap, 0, :, pl.ds(group * width, width)], feats.at[part], sem.at[part]
    )


def weights_kernel(
    groups, scaling, core, feats_hbm, query_hbm, map_hbm, weight_hbm, weights, ordered, stats,
    kept, masks, block_diag, feats, query, value_map, out_weight, sem, side_sem,
):
    taps, _, queries, _ = query.shape
    count = taps * groups
    half = LANES // 2
    each = queries // 2
    sides = [
        [
            pltpu.make_async_copy(whole.at[tap], copied.at[tap], side_sem.at[place, tap])
            for place, (whole, copied) in enumerate(((query_hbm, query), (weight_hbm, out_weight), (map_hbm, value_map)))
        ]
        for tap in range(taps)
    ]
    for tap in range(taps):
        for side in sides[tap]:
            side.start()
    for tap in range(taps):
        for group in range(groups):
            fetched(feats_hbm, feats, sem, groups, tap, group).start()
    kept[...] = jnp.zeros_like(kept)
    mine = core[0]
    row = lax.broadcasted_iota(jnp.int32, (LANES, LANES), 0)
    column = lax.broadcasted_iota(jnp.int32, (LANES, LANES), 1)
    row_head = (row % half) // each
    parity = jnp.where(row < half, mine, 1 - mine)
    order = (column == row_head * queries + 2 * (row % each) + parity).astype(F32).astype(BF16)
    for head in range(GROUP):
        masks[head] = ((column % half) // each == head).astype(F32).astype(BF16)
    def prepare(part):
        tap, group = divmod(part, groups)
        heads = pl.ds(group * GROUP, GROUP)
        asked = lax.dot_general(
            query[tap, heads].reshape(LANES, LANES), order, ROWS_TO_COLUMNS, preferred_element_type=F32
        ).astype(BF16)
        wanted = jnp.dot(
            order, out_weight[tap, heads].reshape(LANES, LANES), preferred_element_type=F32
        ).astype(BF16)
        ordered[part] = wanted
        weighed = lax.dot_general(value_map[tap], wanted, ROWS_BY_COLUMNS, preferred_element_type=F32).astype(BF16)
        spread = block_diag.at[part % 3]
        for head in range(GROUP):
            rows = slice(head * LANES, (head + 1) * LANES)
            spread[rows, :LANES] = asked * masks[head]
            spread[rows, LANES:] = weighed * masks[head]

    for tap in range(taps):
        for side in sides[tap]:
            side.wait()
    for part in range(AHEAD):
        prepare(part)
    for part in range(count):
        fetched(feats_hbm, feats, sem, groups, *divmod(part, groups)).wait()
    for part in range(count):
        both = jnp.dot(feats[part], block_diag[part % 3], preferred_element_type=F32)
        if part + AHEAD < count:
            prepare(part + AHEAD)
        scores = both[:, :LANES] * scaling
        dots = both[:, LANES:]
        top = jnp.max(scores, axis=0, keepdims=True)
        expo = jnp.exp(scores - top)
        total = jnp.sum(expo, axis=0, keepdims=True)
        weighted = jnp.sum(expo * dots, axis=0, keepdims=True)
        tilt = expo * (dots - weighted / total)
        kept[part : part + 1, :] = top
        kept[count + part : count + part + 1, :] = total
        kept[2 * count + part : 2 * count + part + 1, :] = weighted
        weights[part, :, :LANES] = expo.astype(BF16)
        weights[part, :, LANES:] = tilt.astype(BF16)
    found = kept[...]
    found = jnp.where(mine == 0, found, pltpu.roll(found, half, 1))
    stats[...] = jnp.broadcast_to(found[None], stats.shape)


def token_weights(core, features, disc_query, value_map, disc_out, scaling, members):
    taps, heads, queries, head_size = disc_query.shape
    groups = heads // GROUP
    tokens = features.shape[2]
    vmem = pl.BlockSpec(memory_space=pltpu.VMEM)
    return pl.pallas_call(
        functools.partial(weights_kernel, groups, scaling),
        out_shape=(
            jax.ShapeDtypeStruct((taps * groups, tokens, 2 * LANES), BF16),
            jax.ShapeDtypeStruct((taps * groups, LANES, head_size), BF16),
            jax.ShapeDtypeStruct((members, 32, LANES), F32),
        ),
        in_specs=[pl.BlockSpec(memory_space=pltpu.SMEM)] + [pl.BlockSpec(memory_space=pl.ANY)] * 4,
        out_specs=(vmem, vmem, vmem),
        scratch_shapes=[
            pltpu.VMEM((32, LANES), F32),
            pltpu.VMEM((GROUP, LANES, LANES), BF16),
            pltpu.VMEM((3, GROUP * LANES, 2 * LANES), BF16),
            pltpu.VMEM((taps * groups, tokens, GROUP * LANES), BF16),
            pltpu.VMEM(disc_query.shape, BF16),
            pltpu.VMEM(value_map.shape, BF16),
            pltpu.VMEM(disc_out.shape, BF16),
            pltpu.SemaphoreType.DMA((taps * groups,)),
            pltpu.SemaphoreType.DMA((3, taps)),
        ],
        compiler_params=pltpu.CompilerParams(vmem_limit_bytes=VMEM_LARGE),
        cost_estimate=pl.CostEstimate(flops=7 * 10**8, bytes_accessed=4 * 10**6, transcendentals=10**5),
        name="token_weights",
    )(core, features, disc_query, value_map, disc_out)


def pooled_kernel(groups, feats_hbm, weights, sent, stays, feats, sem):
    count = weights.shape[0]
    taps = count // groups
    half = LANES // 2
    each = half // GROUP
    for tap in range(taps):
        for group in range(groups):
            fetched(feats_hbm, feats, sem, groups, tap, group).start()
    for tap in range(taps):
        for group in range(groups):
            fetched(feats_hbm, feats, sem, groups, tap, group).wait()
    for tap in range(taps):
        for group in range(groups):
            part = tap * groups + group
            rows = weights[part].T
            for head in range(GROUP):
                first = slice(head * each, (head + 1) * each)
                second = slice(half + head * each, half + (head + 1) * each)
                found = jnp.dot(
                    jnp.concatenate(
                        [rows[LANES * kind + half * place + head * each :][:each] for kind in range(2) for place in range(2)],
                        axis=0,
                    ),
                    feats[part, :, head * LANES : (head + 1) * LANES],
                    preferred_element_type=F32,
                )
                sent[part, 0, first] = found[:each]
                sent[part, 1, first] = found[each : 2 * each]
                stays[part, first] = found[2 * each : 3 * each]
                sent[part, 2, first] = found[3 * each :]


def pooled_features(features, weights, groups):
    count, tokens, _ = weights.shape
    vmem = pl.BlockSpec(memory_space=pltpu.VMEM)
    return pl.pallas_call(
        functools.partial(pooled_kernel, groups),
        out_shape=(
            jax.ShapeDtypeStruct((count, 3, LANES // 2, LANES), F32),
            jax.ShapeDtypeStruct((count, LANES // 2, LANES), F32),
        ),
        in_specs=[pl.BlockSpec(memory_space=pl.ANY), vmem],
        out_specs=(vmem, vmem),
        scratch_shapes=[
            pltpu.VMEM((count, tokens, GROUP * LANES), BF16),
            pltpu.SemaphoreType.DMA((count,)),
        ],
        compiler_params=pltpu.CompilerParams(vmem_limit_bytes=VMEM_LARGE),
        cost_estimate=pl.CostEstimate(flops=8 * 10**7, bytes_accessed=4 * 10**6, transcendentals=0),
        name="pooled_features",
    )(features, weights)


def joined_kernel(count, member_ref, core, label, every, logit_ref, coefficients):
    half = LANES // 2
    member, mine = member_ref[0], core[0]
    tops = every[:, 0:count]
    top = jnp.max(tops, axis=0)
    factors = jnp.exp(tops - top[None])
    total = jnp.sum(every[:, count : 2 * count] * factors, axis=0)
    centre = jnp.sum(every[:, 2 * count : 3 * count] * factors, axis=0) / total
    logit = jnp.sum(jnp.sum(centre, axis=1, keepdims=True), axis=0, keepdims=True)
    signs = jnp.full((1, 1), 2 * label[0] - 1, jnp.int32).astype(F32)
    slope = -signs * jax.nn.sigmoid(-signs * logit)
    logit_ref[...] = logit
    padding = jnp.zeros((16 - count, LANES), F32)
    for place, of_member in enumerate((member, member + 1 - 2 * mine)):
        seen = every[of_member]
        share = slope * jnp.exp(seen[0:count] - top) / total
        moved = share * (centre - seen[2 * count : 3 * count] / seen[count : 2 * count])
        both = jnp.concatenate([share, padding, moved, padding], axis=0)
        coefficients[place] = jnp.where(mine == 0, both, pltpu.roll(both, half, 1)).T


def joined_stats(member, core, label, every, count):
    vmem = pl.BlockSpec(memory_space=pltpu.VMEM)
    smem = pl.BlockSpec(memory_space=pltpu.SMEM)
    return pl.pallas_call(
        functools.partial(joined_kernel, count),
        out_shape=(
            jax.ShapeDtypeStruct((1, 1), F32),
            jax.ShapeDtypeStruct((2, LANES, 32), F32),
        ),
        in_specs=[smem, smem, smem, vmem],
        out_specs=(vmem, vmem),
        compiler_params=pltpu.CompilerParams(vmem_limit_bytes=VMEM_SMALL),
        cost_estimate=pl.CostEstimate(flops=10**10, bytes_accessed=10**8, transcendentals=10**5),
        name="joined_stats",
    )(member, core, label, every)


def scaled_kernel(groups, scaling, core, own, stays, other, coefficients, ordered, shares, whole):
    count = own.shape[0]
    taps = count // groups
    heads = groups * GROUP
    head_size = own.shape[3]
    half = LANES // 2
    each = half // GROUP
    mine = core[0]
    own_columns = coefficients[0]
    other_columns = coefficients[1]

    def spread(found, part, second):
        return jnp.broadcast_to(found[second * half : (second + 1) * half, part : part + 1], (half, LANES))

    for tap in range(taps):
        grad = jnp.zeros((head_size, head_size), F32)
        for group in range(groups):
            part = tap * groups + group
            first_pool = spread(own_columns, part, 0) * own[part, 0] + spread(other_columns, part, 0) * other[part, 1]
            second_pool = spread(own_columns, part, 1) * own[part, 1] + spread(other_columns, part, 1) * other[part, 0]
            tilt = scaling * (
                (spread(own_columns, part, 0) * stays[part] - spread(own_columns, 16 + part, 0) * own[part, 0])
                + (spread(other_columns, part, 0) * other[part, 2] - spread(other_columns, 16 + part, 0) * other[part, 1])
            )
            pool = jnp.concatenate([first_pool, second_pool], axis=0)
            high = pool.astype(BF16)
            low = (pool - high.astype(F32)).astype(BF16)
            grad = grad + lax.dot_general(high, ordered[part], OVER_ROWS, preferred_element_type=F32)
            grad = grad + lax.dot_general(low, ordered[part], OVER_ROWS, preferred_element_type=F32)
            row = tap * heads + group * GROUP
            for head in range(GROUP):
                rows = slice(head * each, (head + 1) * each)
                shares[0, :, row + head, :] = tilt[rows]
                shares[1, :, row + head, :] = first_pool[rows]
        pieces = shares.shape[1]
        kept = head_size // (2 * pieces)
        whole[tap] = grad.reshape(whole.shape[1:])
        place, second = divmod(tap, 2)
        row = taps * heads + second * kept
        shares[place, :, row : row + kept, :] = whole[tap, :, mine]
    row = taps * heads + kept
    shares[1, :, row:, :] = jnp.zeros((pieces, kept, head_size), F32)


def scaled_shares(core, own, stays, other, coefficients, ordered, taps, pieces, scaling):
    count, _, _, head_size = own.shape
    groups = count // taps
    kept = head_size // (2 * pieces)
    vmem = pl.BlockSpec(memory_space=pltpu.VMEM)
    smem = pl.BlockSpec(memory_space=pltpu.SMEM)
    rows = count * GROUP + 2 * kept
    return pl.pallas_call(
        functools.partial(scaled_kernel, groups, scaling),
        out_shape=jax.ShapeDtypeStruct((2, pieces, rows, head_size), F32),
        in_specs=[smem, vmem, vmem, vmem, vmem, vmem],
        out_specs=vmem,
        scratch_shapes=[pltpu.VMEM((taps, pieces, 2, kept, head_size), F32)],
        compiler_params=pltpu.CompilerParams(vmem_limit_bytes=VMEM_SMALL),
        cost_estimate=pl.CostEstimate(flops=10**8, bytes_accessed=3 * 10**6, transcendentals=10**5),
        name="scaled_shares",
    )(core, own, stays, other, coefficients, ordered)


def summed_kernel(terms, total):
    found = terms[0]
    for term in range(1, terms.shape[0]):
        found = found + terms[term]
    parts, rows, _ = total.shape
    if parts * rows > found.shape[0]:
        found = jnp.concatenate([found, jnp.zeros((parts * rows - found.shape[0], LANES), F32)], axis=0)
    total[...] = found.reshape(total.shape)


def summed_parts(terms, parts):
    rows = -(-terms.shape[1] // (8 * parts)) * 8
    vmem = pl.BlockSpec(memory_space=pltpu.VMEM)
    return pl.pallas_call(
        summed_kernel,
        out_shape=jax.ShapeDtypeStruct((parts, rows, LANES), F32),
        in_specs=[vmem],
        out_specs=vmem,
        compiler_params=pltpu.CompilerParams(vmem_limit_bytes=VMEM_SMALL),
        name="summed_parts",
    )(terms)


def repeated_kernel(terms, total):
    found = terms[0]
    for term in range(1, terms.shape[0]):
        found = found + terms[term]
    total[...] = jnp.broadcast_to(found[None], total.shape)


def repeated_sum(terms, copies):
    vmem = pl.BlockSpec(memory_space=pltpu.VMEM)
    return pl.pallas_call(
        repeated_kernel,
        out_shape=jax.ShapeDtypeStruct((copies, *terms.shape[1:]), F32),
        in_specs=[vmem],
        out_specs=vmem,
        compiler_params=pltpu.CompilerParams(vmem_limit_bytes=VMEM_SMALL),
        name="repeated_sum",
    )(terms)


def final_kernel(gathered, value_map, query_ref, out_ref, map_ref):
    taps, head_size, _ = value_map.shape
    each = query_ref.shape[0] // taps
    kept = map_ref.shape[1]
    parts = gathered.shape[0]
    first = jnp.concatenate([gathered[part, 0] for part in range(parts)], axis=0)
    second = jnp.concatenate([gathered[part, 1] for part in range(parts)], axis=0)
    query_ref[...] = first[: taps * each]
    for tap in range(taps):
        pool = second[tap * each : (tap + 1) * each]
        high = pool.astype(BF16)
        low = (pool - high.astype(F32)).astype(BF16)
        out_ref[tap * each : (tap + 1) * each, :] = jnp.dot(
            high, value_map[tap], preferred_element_type=F32
        ) + jnp.dot(low, value_map[tap], preferred_element_type=F32)
        row = taps * each + (tap % 2) * kept
        map_ref[tap] = (first, second)[tap // 2][row : row + kept]


def final_outputs(gathered, value_map, heads, kept):
    taps, head_size, _ = value_map.shape
    vmem = pl.BlockSpec(memory_space=pltpu.VMEM)
    each = jax.ShapeDtypeStruct((taps * heads, head_size), F32)
    return pl.pallas_call(
        final_kernel,
        out_shape=(each, each, jax.ShapeDtypeStruct((taps, kept, head_size), F32)),
        in_specs=[vmem, vmem],
        out_specs=(vmem, vmem, vmem),
        compiler_params=pltpu.CompilerParams(vmem_limit_bytes=VMEM_SMALL),
        name="final_outputs",
    )(gathered, value_map)


def exchanged(parts, axes):
    return lax.all_to_all(parts, axes, 0, 0)


SEQ = ("yl", "x", "core")
CLIP = ("zh", "zl", "yh")


def on_device(features, disc_query, value_map, disc_out, label):
    taps, heads, queries, head_size = disc_query.shape
    scaling = 0.5 / math.sqrt(head_size)
    members = lax.axis_size(SEQ)
    core = lax.axis_index("core").astype(jnp.int32).reshape(1)
    member = lax.axis_index(SEQ).astype(jnp.int32).reshape(1)
    features, disc_query, disc_out, map_there = (
        pltpu.with_memory_space_constraint(whole, pltpu.HBM) for whole in (features, disc_query, disc_out, value_map)
    )
    weights, ordered, stats = token_weights(core, features, disc_query, map_there, disc_out, scaling, members)
    every = exchanged(stats, SEQ)
    sent, stays = pooled_features(features, weights, heads // GROUP)
    other = lax.ppermute(sent, "core", [(0, 1), (1, 0)])
    logit, coefficients = joined_stats(member, core, label, every, ordered.shape[0])
    shares = scaled_shares(core, sent, stays, other, coefficients, ordered, taps, members // 2, scaling)
    terms = exchanged(shares.reshape(members, -1, head_size), ("yh", "yl", "x"))
    terms = exchanged(summed_parts(terms, lax.axis_size("zl")), ("zl",))
    terms = lax.all_gather(repeated_sum(terms, 1)[0], "zh")
    terms = exchanged(repeated_sum(terms, 2 * lax.axis_size("zl")), ("zl", "yh"))
    gathered = terms.reshape(-1, 2, *terms.shape[1:])
    query_part, out_part, map_part = final_outputs(gathered, value_map, heads, head_size // members)
    return (
        logit.reshape(1),
        query_part.reshape(taps, heads, 1, head_size),
        out_part.reshape(taps, heads, 1, head_size),
        map_part,
    )


def solution(mesh):
    clips, members = mesh.shape["clip"], mesh.shape["seq"]
    near = min(4, clips // 2)
    shape = (clips // (2 * near), near, 2, 2, members // 4, 2)
    inner = Mesh(mesh.devices.reshape(shape), (*CLIP, *SEQ))
    placed = (P(None, CLIP, SEQ, None), P(), P(), P(), P(CLIP))
    return jax.shard_map(
        on_device,
        mesh=inner,
        in_specs=placed,
        out_specs=(P(CLIP), P(None, None, SEQ, None), P(None, None, SEQ, None), P(None, SEQ, None)),
        check_vma=False,
    )
```

```python
import functools
import math

import jax
import jax.numpy as jnp
from jax import lax
from jax.experimental import pallas as pl
from jax.experimental.pallas import tpu as pltpu
from jax.sharding import Mesh, PartitionSpec as P

LANES = 128
GROUP = 8
F32 = jnp.float32
BF16 = jnp.bfloat16
ROWS_BY_COLUMNS = (((1,), (1,)), ((), ()))
AHEAD = 3
VMEM_LARGE = 16 * 2**20
VMEM_SMALL = 16 * 2**20
ROWS_TO_COLUMNS = (((0,), (1,)), ((), ()))
OVER_ROWS = (((0,), (0,)), ((), ()))


def fetched(feats_hbm, feats, sem, groups, tap, group):
    width = GROUP * LANES
    part = tap * groups + group
    return pltpu.make_async_copy(
        feats_hbm.at[tap, 0, :, pl.ds(group * width, width)], feats.at[part], sem.at[part]
    )


def weights_kernel(
    groups, scaling, member, label, feats_hbm, query_hbm, map_hbm, weight_hbm, weights, ordered, stats,
    kept, masks, block_diag, feats, query, value_map, out_weight, sem, side_sem,
):
    taps, _, queries, _ = query.shape
    count = taps * groups
    half = LANES // 2
    each = queries // 2
    sides = [
        [
            pltpu.make_async_copy(whole.at[tap], copied.at[tap], side_sem.at[place, tap])
            for place, (whole, copied) in enumerate(((query_hbm, query), (weight_hbm, out_weight), (map_hbm, value_map)))
        ]
        for tap in range(taps)
    ]
    for tap in range(taps):
        for side in sides[tap]:
            side.start()
    for tap in range(taps):
        for group in range(groups):
            fetched(feats_hbm, feats, sem, groups, tap, group).start()
    kept[...] = jnp.zeros_like(kept)
    mine = lax.rem(member[0], 2)
    row = lax.broadcasted_iota(jnp.int32, (LANES, LANES), 0)
    column = lax.broadcasted_iota(jnp.int32, (LANES, LANES), 1)
    row_head = (row % half) // each
    parity = jnp.where(row < half, mine, 1 - mine)
    order = (column == row_head * queries + 2 * (row % each) + parity).astype(F32).astype(BF16)
    for head in range(GROUP):
        masks[head] = ((column % half) // each == head).astype(F32).astype(BF16)
    def prepare(part):
        tap, group = divmod(part, groups)
        heads = pl.ds(group * GROUP, GROUP)
        asked = lax.dot_general(
            query[tap, heads].reshape(LANES, LANES), order, ROWS_TO_COLUMNS, preferred_element_type=F32
        ).astype(BF16)
        wanted = jnp.dot(
            order, out_weight[tap, heads].reshape(LANES, LANES), preferred_element_type=F32
        ).astype(BF16)
        ordered[part] = wanted
        weighed = lax.dot_general(value_map[tap], wanted, ROWS_BY_COLUMNS, preferred_element_type=F32).astype(BF16)
        spread = block_diag.at[part % 3]
        for head in range(GROUP):
            rows = slice(head * LANES, (head + 1) * LANES)
            spread[rows, :LANES] = asked * masks[head]
            spread[rows, LANES:] = weighed * masks[head]

    for tap in range(taps):
        for side in sides[tap]:
            side.wait()
    for part in range(AHEAD):
        prepare(part)
    for part in range(count):
        fetched(feats_hbm, feats, sem, groups, *divmod(part, groups)).wait()
    for part in range(count):
        both = jnp.dot(feats[part], block_diag[part % 3], preferred_element_type=F32)
        if part + AHEAD < count:
            prepare(part + AHEAD)
        scores = both[:, :LANES] * scaling
        dots = both[:, LANES:]
        top = jnp.max(scores, axis=0, keepdims=True)
        expo = jnp.exp(scores - top)
        total = jnp.sum(expo, axis=0, keepdims=True)
        weighted = jnp.sum(expo * dots, axis=0, keepdims=True)
        tilt = expo * (dots - weighted / total)
        kept[part : part + 1, :] = top
        kept[count + part : count + part + 1, :] = total
        kept[2 * count + part : 2 * count + part + 1, :] = weighted
        weights[part, :, :LANES] = expo.astype(BF16)
        weights[part, :, LANES:] = tilt.astype(BF16)
    found = kept[...]
    found = jnp.where(mine == 0, found, pltpu.roll(found, half, 1))
    stats[...] = jnp.broadcast_to(found[None], stats.shape)


def token_weights(member, label, features, disc_query, value_map, disc_out, scaling, members):
    taps, heads, queries, head_size = disc_query.shape
    groups = heads // GROUP
    tokens = features.shape[2]
    vmem = pl.BlockSpec(memory_space=pltpu.VMEM)
    return pl.pallas_call(
        functools.partial(weights_kernel, groups, scaling),
        out_shape=(
            jax.ShapeDtypeStruct((taps * groups, tokens, 2 * LANES), BF16),
            jax.ShapeDtypeStruct((taps * groups, LANES, head_size), BF16),
            jax.ShapeDtypeStruct((members, 32, LANES), F32),
        ),
        in_specs=[pl.BlockSpec(memory_space=pltpu.SMEM)] * 2 + [pl.BlockSpec(memory_space=pl.ANY)] * 4,
        out_specs=(vmem, vmem, vmem),
        scratch_shapes=[
            pltpu.VMEM((32, LANES), F32),
            pltpu.VMEM((GROUP, LANES, LANES), BF16),
            pltpu.VMEM((3, GROUP * LANES, 2 * LANES), BF16),
            pltpu.VMEM((taps * groups, tokens, GROUP * LANES), BF16),
            pltpu.VMEM(disc_query.shape, BF16),
            pltpu.VMEM(value_map.shape, BF16),
            pltpu.VMEM(disc_out.shape, BF16),
            pltpu.SemaphoreType.DMA((taps * groups,)),
            pltpu.SemaphoreType.DMA((3, taps)),
        ],
        compiler_params=pltpu.CompilerParams(vmem_limit_bytes=VMEM_LARGE),
        cost_estimate=pl.CostEstimate(flops=7 * 10**8, bytes_accessed=4 * 10**6, transcendentals=10**5),
        name="token_weights",
    )(member, label, features, disc_query, value_map, disc_out)


def pooled_kernel(groups, feats_hbm, weights, sent, stays, feats, sem):
    count = weights.shape[0]
    taps = count // groups
    half = LANES // 2
    each = half // GROUP
    for tap in range(taps):
        for group in range(groups):
            fetched(feats_hbm, feats, sem, groups, tap, group).start()
    for tap in range(taps):
        for group in range(groups):
            fetched(feats_hbm, feats, sem, groups, tap, group).wait()
    for tap in range(taps):
        for group in range(groups):
            part = tap * groups + group
            rows = weights[part].T
            for head in range(GROUP):
                first = slice(head * each, (head + 1) * each)
                second = slice(half + head * each, half + (head + 1) * each)
                found = jnp.dot(
                    jnp.concatenate(
                        [rows[LANES * kind + half * place + head * each :][:each] for kind in range(2) for place in range(2)],
                        axis=0,
                    ),
                    feats[part, :, head * LANES : (head + 1) * LANES],
                    preferred_element_type=F32,
                )
                sent[part, 0, first] = found[:each]
                sent[part, 1, first] = found[each : 2 * each]
                stays[part, first] = found[2 * each : 3 * each]
                sent[part, 2, first] = found[3 * each :]


def pooled_features(features, weights, groups):
    count, tokens, _ = weights.shape
    vmem = pl.BlockSpec(memory_space=pltpu.VMEM)
    return pl.pallas_call(
        functools.partial(pooled_kernel, groups),
        out_shape=(
            jax.ShapeDtypeStruct((count, 3, LANES // 2, LANES), F32),
            jax.ShapeDtypeStruct((count, LANES // 2, LANES), F32),
        ),
        in_specs=[pl.BlockSpec(memory_space=pl.ANY), vmem],
        out_specs=(vmem, vmem),
        scratch_shapes=[
            pltpu.VMEM((count, tokens, GROUP * LANES), BF16),
            pltpu.SemaphoreType.DMA((count,)),
        ],
        compiler_params=pltpu.CompilerParams(vmem_limit_bytes=VMEM_LARGE),
        cost_estimate=pl.CostEstimate(flops=8 * 10**7, bytes_accessed=4 * 10**6, transcendentals=0),
        name="pooled_features",
    )(features, weights)


def joined_kernel(count, member_ref, label, every, logit_ref, coefficients):
    half = LANES // 2
    member = member_ref[0]
    mine = lax.rem(member, 2)
    tops = every[:, 0:count]
    top = jnp.max(tops, axis=0)
    factors = jnp.exp(tops - top[None])
    total = jnp.sum(every[:, count : 2 * count] * factors, axis=0)
    centre = jnp.sum(every[:, 2 * count : 3 * count] * factors, axis=0) / total
    logit = jnp.sum(jnp.sum(centre, axis=1, keepdims=True), axis=0, keepdims=True)
    signs = jnp.full((1, 1), 2 * label[0] - 1, jnp.int32).astype(F32)
    slope = -signs * jax.nn.sigmoid(-signs * logit)
    logit_ref[...] = logit
    padding = jnp.zeros((16 - count, LANES), F32)
    for place, of_member in enumerate((member, member + 1 - 2 * mine)):
        seen = every[of_member]
        share = slope * jnp.exp(seen[0:count] - top) / total
        moved = share * (centre - seen[2 * count : 3 * count] / seen[count : 2 * count])
        both = jnp.concatenate([share, padding, moved, padding], axis=0)
        coefficients[place] = jnp.where(mine == 0, both, pltpu.roll(both, half, 1)).T


def joined_stats(member, label, every, count):
    vmem = pl.BlockSpec(memory_space=pltpu.VMEM)
    smem = pl.BlockSpec(memory_space=pltpu.SMEM)
    return pl.pallas_call(
        functools.partial(joined_kernel, count),
        out_shape=(
            jax.ShapeDtypeStruct((1, 1), F32),
            jax.ShapeDtypeStruct((2, LANES, 32), F32),
        ),
        in_specs=[smem, smem, vmem],
        out_specs=(vmem, vmem),
        compiler_params=pltpu.CompilerParams(vmem_limit_bytes=VMEM_SMALL),
        cost_estimate=pl.CostEstimate(flops=10**10, bytes_accessed=10**8, transcendentals=10**5),
        name="joined_stats",
    )(member, label, every)


def scaled_kernel(groups, scaling, member, own, stays, other, coefficients, ordered, shares, whole):
    count = own.shape[0]
    taps = count // groups
    heads = groups * GROUP
    head_size = own.shape[3]
    half = LANES // 2
    each = half // GROUP
    mine = lax.rem(member[0], 2)
    own_columns = coefficients[0]
    other_columns = coefficients[1]

    def spread(found, part, second):
        return jnp.broadcast_to(found[second * half : (second + 1) * half, part : part + 1], (half, LANES))

    for tap in range(taps):
        grad = jnp.zeros((head_size, head_size), F32)
        for group in range(groups):
            part = tap * groups + group
            first_pool = spread(own_columns, part, 0) * own[part, 0] + spread(other_columns, part, 0) * other[part, 1]
            second_pool = spread(own_columns, part, 1) * own[part, 1] + spread(other_columns, part, 1) * other[part, 0]
            tilt = scaling * (
                (spread(own_columns, part, 0) * stays[part] - spread(own_columns, 16 + part, 0) * own[part, 0])
                + (spread(other_columns, part, 0) * other[part, 2] - spread(other_columns, 16 + part, 0) * other[part, 1])
            )
            pool = jnp.concatenate([first_pool, second_pool], axis=0)
            high = pool.astype(BF16)
            low = (pool - high.astype(F32)).astype(BF16)
            grad = grad + lax.dot_general(high, ordered[part], OVER_ROWS, preferred_element_type=F32)
            grad = grad + lax.dot_general(low, ordered[part], OVER_ROWS, preferred_element_type=F32)
            row = tap * heads + group * GROUP
            for head in range(GROUP):
                rows = slice(head * each, (head + 1) * each)
                shares[0, :, row + head, :] = tilt[rows]
                shares[1, :, row + head, :] = first_pool[rows]
        pieces = shares.shape[1]
        kept = head_size // (2 * pieces)
        whole[tap] = grad.reshape(whole.shape[1:])
        place, second = divmod(tap, 2)
        row = taps * heads + second * kept
        shares[place, :, row : row + kept, :] = whole[tap, :, mine]
    row = taps * heads + kept
    shares[1, :, row:, :] = jnp.zeros((pieces, kept, head_size), F32)


def scaled_shares(member, own, stays, other, coefficients, ordered, taps, pieces, scaling):
    count, _, _, head_size = own.shape
    groups = count // taps
    kept = head_size // (2 * pieces)
    vmem = pl.BlockSpec(memory_space=pltpu.VMEM)
    smem = pl.BlockSpec(memory_space=pltpu.SMEM)
    rows = count * GROUP + 2 * kept
    return pl.pallas_call(
        functools.partial(scaled_kernel, groups, scaling),
        out_shape=jax.ShapeDtypeStruct((2, pieces, rows, head_size), F32),
        in_specs=[smem, vmem, vmem, vmem, vmem, vmem],
        out_specs=vmem,
        scratch_shapes=[pltpu.VMEM((taps, pieces, 2, kept, head_size), F32)],
        compiler_params=pltpu.CompilerParams(vmem_limit_bytes=VMEM_SMALL),
        cost_estimate=pl.CostEstimate(flops=10**8, bytes_accessed=3 * 10**6, transcendentals=10**5),
        name="scaled_shares",
    )(member, own, stays, other, coefficients, ordered)


def summed_kernel(terms, total):
    found = terms[0]
    for term in range(1, terms.shape[0]):
        found = found + terms[term]
    parts, rows, _ = total.shape
    if parts * rows > found.shape[0]:
        found = jnp.concatenate([found, jnp.zeros((parts * rows - found.shape[0], LANES), F32)], axis=0)
    total[...] = found.reshape(total.shape)


def summed_parts(terms, parts):
    rows = -(-terms.shape[1] // (8 * parts)) * 8
    vmem = pl.BlockSpec(memory_space=pltpu.VMEM)
    return pl.pallas_call(
        summed_kernel,
        out_shape=jax.ShapeDtypeStruct((parts, rows, LANES), F32),
        in_specs=[vmem],
        out_specs=vmem,
        compiler_params=pltpu.CompilerParams(vmem_limit_bytes=VMEM_SMALL),
        name="summed_parts",
    )(terms)


def repeated_kernel(terms, total):
    found = terms[0]
    for term in range(1, terms.shape[0]):
        found = found + terms[term]
    total[...] = jnp.broadcast_to(found[None], total.shape)


def repeated_sum(terms, copies):
    vmem = pl.BlockSpec(memory_space=pltpu.VMEM)
    return pl.pallas_call(
        repeated_kernel,
        out_shape=jax.ShapeDtypeStruct((copies, *terms.shape[1:]), F32),
        in_specs=[vmem],
        out_specs=vmem,
        compiler_params=pltpu.CompilerParams(vmem_limit_bytes=VMEM_SMALL),
        name="repeated_sum",
    )(terms)


def final_kernel(gathered, value_map, query_ref, out_ref, map_ref):
    taps, head_size, _ = value_map.shape
    each = query_ref.shape[0] // taps
    kept = map_ref.shape[1]
    parts = gathered.shape[0]
    first = jnp.concatenate([gathered[part, 0] for part in range(parts)], axis=0)
    second = jnp.concatenate([gathered[part, 1] for part in range(parts)], axis=0)
    query_ref[...] = first[: taps * each]
    for tap in range(taps):
        pool = second[tap * each : (tap + 1) * each]
        high = pool.astype(BF16)
        low = (pool - high.astype(F32)).astype(BF16)
        out_ref[tap * each : (tap + 1) * each, :] = jnp.dot(
            high, value_map[tap], preferred_element_type=F32
        ) + jnp.dot(low, value_map[tap], preferred_element_type=F32)
        row = taps * each + (tap % 2) * kept
        map_ref[tap] = (first, second)[tap // 2][row : row + kept]


def final_outputs(gathered, value_map, heads, kept):
    taps, head_size, _ = value_map.shape
    vmem = pl.BlockSpec(memory_space=pltpu.VMEM)
    each = jax.ShapeDtypeStruct((taps * heads, head_size), F32)
    return pl.pallas_call(
        final_kernel,
        out_shape=(each, each, jax.ShapeDtypeStruct((taps, kept, head_size), F32)),
        in_specs=[vmem, vmem],
        out_specs=(vmem, vmem, vmem),
        compiler_params=pltpu.CompilerParams(vmem_limit_bytes=VMEM_SMALL),
        name="final_outputs",
    )(gathered, value_map)


def exchanged(parts, axes):
    return lax.all_to_all(parts, axes, 0, 0)


SEQ = ("yl", "x", "core")
CLIP = ("zh", "zl", "yh")


def on_device(features, disc_query, value_map, disc_out, label):
    taps, heads, queries, head_size = disc_query.shape
    scaling = 0.5 / math.sqrt(head_size)
    members = lax.axis_size(SEQ)
    member = lax.axis_index(SEQ).astype(jnp.int32).reshape(1)
    features, disc_query, disc_out, map_there = (
        pltpu.with_memory_space_constraint(whole, pltpu.HBM) for whole in (features, disc_query, disc_out, value_map)
    )
    weights, ordered, stats = token_weights(member, label, features, disc_query, map_there, disc_out, scaling, members)
    every = exchanged(stats, SEQ)
    sent, stays = pooled_features(features, weights, heads // GROUP)
    other = lax.ppermute(sent, "core", [(0, 1), (1, 0)])
    logit, coefficients = joined_stats(member, label, every, ordered.shape[0])
    shares = scaled_shares(member, sent, stays, other, coefficients, ordered, taps, members // 2, scaling)
    terms = exchanged(shares.reshape(members, -1, head_size), ("yh", "yl", "x"))
    terms = exchanged(summed_parts(terms, lax.axis_size("zl")), ("zl",))
    terms = lax.all_gather(repeated_sum(terms, 1)[0], "zh")
    terms = exchanged(repeated_sum(terms, 2 * lax.axis_size("zl")), ("zl", "yh"))
    gathered = terms.reshape(-1, 2, *terms.shape[1:])
    query_part, out_part, map_part = final_outputs(gathered, value_map, heads, head_size // members)
    return (
        logit.reshape(1),
        query_part.reshape(taps, heads, 1, head_size),
        out_part.reshape(taps, heads, 1, head_size),
        map_part,
    )


def solution(mesh):
    clips, members = mesh.shape["clip"], mesh.shape["seq"]
    near = min(4, clips // 2)
    shape = (clips // (2 * near), near, 2, 2, members // 4, 2)
    inner = Mesh(mesh.devices.reshape(shape), (*CLIP, *SEQ))
    placed = (P(None, CLIP, SEQ, None), P(), P(), P(), P(CLIP))
    return jax.shard_map(
        on_device,
        mesh=inner,
        in_specs=placed,
        out_specs=(P(CLIP), P(None, None, SEQ, None), P(None, None, SEQ, None), P(None, SEQ, None)),
        check_vma=False,
    )
```
